32 devices in a mesh: seq: 8 (over z, x), ch: 4 (over y, core).
Axes of the slice: x: 2, y: 2, z: 4, core: 2. Of those that a mesh axis runs over, the one named last changes fastest.
Arguments:
- query_raw: bfloat16 [1024, 2048], P('seq', 'ch'), may hold values from -6 to 6
- key_raw: bfloat16 [1024, 2048], P('seq', 'ch'), may hold values from -6 to 6
- value_raw: bfloat16 [1024, 2048], P('seq', 'ch'), may hold values from -6 to 6
- featurizer: float32 [3, 7, 2048], P(None, None, 'ch'), may hold values from -2 to 2
- filter_taps: bfloat16 [1024, 2048], P(('seq', 'ch')), may hold values from -2.5 to 2.5
- cotangent: bfloat16 [1024, 2048], P('seq', 'ch'), may hold values from -6 to 6
Outputs:
- mixed: bfloat16 [1024, 2048], P('seq', 'ch')
- query_grad: bfloat16 [1024, 2048], P('seq', 'ch')
- key_grad: bfloat16 [1024, 2048], P('seq', 'ch')
- value_grad: bfloat16 [1024, 2048], P('seq', 'ch')
- filter_grad: float32 [1024, 2048], P(('seq', 'ch'))
- featurizer_grad: float32 [3, 7, 2048], P(None, None, 'ch')
The draws below stay inside these ranges and needn't reach their ends.
All inputs are finite; a program needn't handle non-finite values.
Results may differ from the reference program's by a relative error of at most 0.0085.
Values may be sent and summed in bfloat16 or wider, within the bound.
A program may use at most 64 MiB of HBM per device.

```python
import math
import jax
import jax.numpy as jnp
from jax import lax

D = 2048
TAPS = 7
TOKENS = 1024


def draw_filter_taps(key, part):
    base = jax.random.fold_in(key, 7)
    noise_key, rate_key, pick_key, amp_key = jax.random.split(base, 4)
    positions = jnp.arange(TOKENS, dtype=jnp.float32)
    slow_rate = math.log(10.0) / TOKENS
    slow_rates = slow_rate * jnp.exp(jax.random.uniform(rate_key, (D,), jnp.float32, math.log(0.25), 0.0))
    fast_rates = jnp.exp(jax.random.uniform(jax.random.fold_in(rate_key, 3), (D,), jnp.float32, math.log(1.0 / 50.0), math.log(1.0 / 30.0)))
    picked = jax.random.bernoulli(pick_key, 0.5, (D,))
    rates = jnp.where(picked, slow_rates, fast_rates)
    noise = jax.random.truncated_normal(noise_key, -4.0, 4.0, (TOKENS, D), jnp.float32)
    amplitude = jnp.sqrt((1.0 - jnp.exp(-2.0 * rates)) / (1.0 - jnp.exp(-2.0 * rates * TOKENS)))
    amplitude = amplitude * jnp.exp(jax.random.uniform(amp_key, (D,), jnp.float32, math.log(0.5), math.log(2.0)))
    taps = noise * amplitude[None, :] * jnp.exp(-rates[None, :] * positions[:, None])
    return taps.astype(jnp.bfloat16)


def levels(own_key, shape, pieces, least, top_value):
    factor_of = 1.0
    for dim, shards_of in pieces:
        draws = jax.random.uniform(jax.random.fold_in(jax.random.fold_in(own_key, 6), dim), (shards_of,), jnp.float32, least / len(pieces), top_value / len(pieces))
        factor_of = factor_of * jnp.repeat(jnp.exp(draws), shape[dim] // shards_of).reshape((-1,) + (1,) * (len(shape) - 1 - dim))
    return factor_of


def normal_values(own_key, dims, spread, bound, cuts=(), kind=jnp.bfloat16):
    entries = spread * jax.random.normal(own_key, dims, jnp.float32)
    if cuts:
        entries = entries * levels(own_key, dims, cuts, -0.22, 0.18)
    return jnp.clip(entries, -bound, bound).astype(kind)


def setup_inputs(seed: int = 0) -> dict:
    splits = jax.random.split(jax.random.key(seed), 7)
    query_raw = normal_values(splits[0], (TOKENS, D), 1.0, 6.0, ((0, 8), (1, 4)))
    key_raw = normal_values(splits[1], (TOKENS, D), 1.0, 6.0, ((0, 8), (1, 4)))
    value_raw = normal_values(splits[2], (TOKENS, D), 1.0, 6.0, ((0, 8), (1, 4)))
    featurizer = normal_values(splits[3], (3, TAPS, D), TAPS ** -0.5, 2.0, ((2, 4),), jnp.float32)
    filter_taps = draw_filter_taps(jax.random.fold_in(splits[6], 71), 0)
    cotangent = normal_values(splits[5], (TOKENS, D), 1.0, 6.0, ((0, 8), (1, 4)))
    return {"query_raw": query_raw, "key_raw": key_raw, "value_raw": value_raw, "featurizer": featurizer, "filter_taps": filter_taps, "cotangent": cotangent}


def featurize(raw, weight):
    signal = raw.astype(jnp.float32)
    padded = jnp.pad(signal, ((TAPS - 1, 0), (0, 0)))
    total = jnp.zeros_like(signal)
    for lag_index in range(TAPS):
        start = TAPS - 1 - lag_index
        total = total + weight[lag_index][None, :] * padded[start:start + TOKENS]
    return total


def unfeaturize(grad, weight):
    padded = jnp.pad(grad, ((0, TAPS - 1), (0, 0)))
    total = jnp.zeros_like(grad)
    for lag_index in range(TAPS):
        total = total + weight[lag_index][None, :] * padded[lag_index:lag_index + TOKENS]
    return total


def weight_terms(grad, raw):
    padded = jnp.pad(raw.astype(jnp.float32), ((TAPS - 1, 0), (0, 0)))
    terms = []
    for lag_index in range(TAPS):
        start = TAPS - 1 - lag_index
        terms.append(jnp.sum(grad * padded[start:start + TOKENS], axis=0))
    return jnp.stack(terms)


def reference(query_raw, key_raw, value_raw, featurizer, filter_taps, cotangent):
    feat_query = featurize(query_raw, featurizer[0])
    feat_key = featurize(key_raw, featurizer[1])
    feat_value = featurize(value_raw, featurizer[2])
    mixer = (feat_key * feat_value).astype(jnp.bfloat16)
    upstream = cotangent.astype(jnp.float32)
    gate = (upstream * feat_query).astype(jnp.bfloat16)
    block_width = math.gcd(D, 256)
    full_len = 2 * TOKENS

    def to_blocks(array):
        return array.astype(jnp.float32).T.reshape(D // block_width, block_width, TOKENS)

    def from_blocks(array):
        return array.reshape(D, TOKENS).T

    def per_block(items):
        mix_block, taps_block, gate_block = items
        mix_spec = jnp.fft.rfft(mix_block, n=full_len, axis=-1)
        taps_spec = jnp.fft.rfft(taps_block, n=full_len, axis=-1)
        gate_spec = jnp.fft.rfft(gate_block, n=full_len, axis=-1)
        conv_block = jnp.fft.irfft(taps_spec * mix_spec, n=full_len, axis=-1)[:, :TOKENS]
        mix_grad_block = jnp.fft.irfft(jnp.conj(taps_spec) * gate_spec, n=full_len, axis=-1)[:, :TOKENS]
        taps_grad_block = jnp.fft.irfft(jnp.conj(mix_spec) * gate_spec, n=full_len, axis=-1)[:, :TOKENS]
        return conv_block, mix_grad_block, taps_grad_block

    conv, mixer_grad, taps_grad = lax.map(per_block, (to_blocks(mixer), to_blocks(filter_taps), to_blocks(gate)))
    scale = TOKENS ** -0.5
    conv = from_blocks(conv).astype(jnp.bfloat16)
    mixer_grad = from_blocks(mixer_grad).astype(jnp.bfloat16)
    filter_grad = from_blocks(taps_grad).astype(jnp.float32) * scale
    conv_float = conv.astype(jnp.float32)
    mixed = (feat_query * conv_float).astype(jnp.bfloat16)
    mix_grad_float = mixer_grad.astype(jnp.float32)
    query_feat_grad = upstream * conv_float
    key_feat_grad = mix_grad_float * feat_value
    value_feat_grad = mix_grad_float * feat_key
    query_grad = unfeaturize(query_feat_grad, featurizer[0]).astype(jnp.bfloat16)
    key_grad = unfeaturize(key_feat_grad, featurizer[1]).astype(jnp.bfloat16)
    value_grad = unfeaturize(value_feat_grad, featurizer[2]).astype(jnp.bfloat16)
    featurizer_grad = jnp.stack([
        weight_terms(query_feat_grad, query_raw),
        weight_terms(key_feat_grad, key_raw),
        weight_terms(value_feat_grad, value_raw),
    ]) * scale
    return mixed, query_grad, key_grad, value_grad, filter_grad, featurizer_grad
```

```python
import functools
import math

import jax
import jax.numpy as jnp
import numpy as np
from jax import lax
from jax.experimental import pallas as pl
from jax.experimental.pallas import tpu as pltpu
from jax.sharding import PartitionSpec as P

TAPS = 7


exact_mode = lax.Precision.HIGHEST


def passed_along(value, axis, steps):
    count = lax.axis_size(axis)
    initial, last = (max(0, -steps), min(count, count - steps))
    return lax.ppermute(value, axis, [(source, source + steps) for source in range(initial, last)])


def spectrum_tables(half_rows, tile_width):
    full_rows = 2 * half_rows
    length_full = full_rows * tile_width
    row_index = jnp.arange(full_rows, dtype=jnp.int32)
    col_index = jnp.arange(tile_width, dtype=jnp.int32)
    outer_angle = (
        2.0
        * math.pi
        / full_rows
        * (row_index[:, None] * row_index[None, :] % full_rows).astype(jnp.float32)
    )
    twist_angle = (
        2.0
        * math.pi
        / length_full
        * (row_index[:, None] * col_index[None, :] % length_full).astype(jnp.float32)
    )
    inner_angle = (
        2.0
        * math.pi
        / tile_width
        * (col_index[:, None] * col_index[None, :] % tile_width).astype(jnp.float32)
    )
    return (
        jnp.cos(outer_angle),
        -jnp.sin(outer_angle),
        jnp.cos(twist_angle),
        -jnp.sin(twist_angle),
        jnp.cos(inner_angle),
        -jnp.sin(inner_angle),
    )


def right_product(left, table):
    return jnp.einsum("ckm,mj->ckj", left, table, precision=exact_mode)


def to_spectrum(signal, tables):
    outer_re, outer_im, twist_re, twist_im, inner_re, inner_im = tables
    half_rows = outer_re.shape[0] // 2
    tile_width = inner_re.shape[0]
    blocks = signal.reshape(signal.shape[0], half_rows, tile_width)
    section_re = jnp.einsum("kn,cnm->ckm", outer_re[:, :half_rows], blocks, precision=exact_mode)
    section_im = jnp.einsum("kn,cnm->ckm", outer_im[:, :half_rows], blocks, precision=exact_mode)
    turned_re = section_re * twist_re - section_im * twist_im
    turned_im = section_re * twist_im + section_im * twist_re
    spec_re = right_product(turned_re, inner_re) - right_product(turned_im, inner_im)
    spec_im = right_product(turned_re, inner_im) + right_product(turned_im, inner_re)
    return (spec_re, spec_im)


def from_spectrum(spectrum, tables):
    outer_re, outer_im, twist_re, twist_im, inner_re, inner_im = tables
    half_rows = outer_re.shape[0] // 2
    tile_width = inner_re.shape[0]
    spec_re, spec_im = spectrum
    back_re = right_product(spec_re, inner_re) + right_product(spec_im, inner_im)
    back_im = right_product(spec_im, inner_re) - right_product(spec_re, inner_im)
    untwist_re = back_re * twist_re + back_im * twist_im
    untwist_im = back_im * twist_re - back_re * twist_im
    signal = jnp.einsum("nk,ckm->cnm", outer_re[:half_rows], untwist_re, precision=exact_mode)
    signal = signal + jnp.einsum(
        "nk,ckm->cnm", outer_im[:half_rows], untwist_im, precision=exact_mode
    )
    return signal.reshape(signal.shape[0], half_rows * tile_width) / (2.0 * half_rows * tile_width)


def times_spectrum(first, second):
    return (
        first[0] * second[0] - first[1] * second[1],
        first[0] * second[1] + first[1] * second[0],
    )


def conj_times(first, second):
    return (
        first[0] * second[0] + first[1] * second[1],
        first[0] * second[1] - first[1] * second[0],
    )


def featurize(padded, weight, tok_rows):
    total = jnp.zeros((tok_rows, padded.shape[1]), jnp.float32)
    for lag_index in range(TAPS):
        start = TAPS - 1 - lag_index
        total = total + weight[lag_index][None, :] * padded[start : start + tok_rows]
    return total


def unfeaturize(extended, weight, tok_rows):
    total = jnp.zeros((tok_rows, extended.shape[1]), jnp.float32)
    for lag_index in range(TAPS):
        total = total + weight[lag_index][None, :] * extended[lag_index : lag_index + tok_rows]
    return total


def weight_terms(grad, padded, tok_rows):
    terms = []
    for lag_index in range(TAPS):
        start = TAPS - 1 - lag_index
        terms.append(jnp.sum(grad * padded[start : start + tok_rows], axis=0))
    return jnp.stack(terms)


def on_device_large(query_raw, key_raw, value_raw, featurizer, filter_taps, cotangent):
    tok_rows = query_raw.shape[0]
    lag_rows = TAPS - 1
    cut_start = tok_rows - lag_rows
    seq_count = lax.axis_size("seq")
    ch_count = lax.axis_size("ch")
    rim_query, rim_key, rim_value = passed_along(
        (query_raw[cut_start:], key_raw[cut_start:], value_raw[cut_start:]), "seq", 1
    )
    padded_query = jnp.concatenate([rim_query, query_raw], axis=0).astype(jnp.float32)
    padded_key = jnp.concatenate([rim_key, key_raw], axis=0).astype(jnp.float32)
    padded_value = jnp.concatenate([rim_value, value_raw], axis=0).astype(jnp.float32)
    feat_query = featurize(padded_query, featurizer[0], tok_rows)
    feat_key = featurize(padded_key, featurizer[1], tok_rows)
    feat_value = featurize(padded_value, featurizer[2], tok_rows)
    mixer = (feat_key * feat_value).astype(jnp.bfloat16)
    mix_cols = lax.all_to_all(mixer.T, "seq", split_axis=0, concat_axis=1, tiled=True)
    chan_total, row_part = (filter_taps.shape[1], filter_taps.shape[0])
    block_width = chan_total // (seq_count * ch_count)
    ordered = filter_taps.T.reshape(ch_count, seq_count, block_width, row_part)
    ordered = jnp.transpose(ordered, (1, 0, 2, 3)).reshape(chan_total, row_part)
    taps_cols = lax.all_to_all(ordered, ("seq", "ch"), split_axis=0, concat_axis=1, tiled=True)
    length_full = mix_cols.shape[1]
    tables = spectrum_tables(length_full // 128, 128)
    mix_spec = to_spectrum(mix_cols.astype(jnp.float32), tables)
    taps_spec = to_spectrum(taps_cols.astype(jnp.float32), tables)
    conv_cols = from_spectrum(times_spectrum(taps_spec, mix_spec), tables).astype(jnp.bfloat16)
    conv_rows = lax.all_to_all(conv_cols, "seq", split_axis=1, concat_axis=0, tiled=True).T
    conv_float = conv_rows.astype(jnp.float32)
    mixed = (feat_query * conv_float).astype(jnp.bfloat16)
    upstream = cotangent.astype(jnp.float32)
    gate = (upstream * feat_query).astype(jnp.bfloat16)
    gate_cols = lax.all_to_all(gate.T, "seq", split_axis=0, concat_axis=1, tiled=True)
    gate_spec = to_spectrum(gate_cols.astype(jnp.float32), tables)
    scale = length_full ** (-0.5)
    mix_grad_cols = from_spectrum(conj_times(taps_spec, gate_spec), tables).astype(jnp.bfloat16)
    taps_grad_cols = from_spectrum(conj_times(mix_spec, gate_spec), tables) * scale
    mix_back = lax.all_to_all(mix_grad_cols, "seq", split_axis=1, concat_axis=0, tiled=True)
    mix_grad_float = mix_back.T.astype(jnp.float32)
    joint_back = lax.all_to_all(
        taps_grad_cols, ("seq", "ch"), split_axis=1, concat_axis=0, tiled=True
    )
    block_width = joint_back.shape[0] // (seq_count * ch_count)
    row_part = joint_back.shape[1]
    unordered = joint_back.reshape(seq_count, ch_count, block_width, row_part)
    unordered = jnp.transpose(unordered, (1, 0, 2, 3)).reshape(joint_back.shape[0], row_part)
    filter_grad = unordered.T
    query_feat_grad = upstream * conv_float
    key_feat_grad = mix_grad_float * feat_value
    value_feat_grad = mix_grad_float * feat_key
    next_query, next_key, next_value = passed_along(
        (query_feat_grad[:lag_rows], key_feat_grad[:lag_rows], value_feat_grad[:lag_rows]),
        "seq",
        -1,
    )
    query_grad = unfeaturize(
        jnp.concatenate([query_feat_grad, next_query], axis=0), featurizer[0], tok_rows
    )
    key_grad = unfeaturize(
        jnp.concatenate([key_feat_grad, next_key], axis=0), featurizer[1], tok_rows
    )
    value_grad = unfeaturize(
        jnp.concatenate([value_feat_grad, next_value], axis=0), featurizer[2], tok_rows
    )
    partial_terms = jnp.stack(
        [
            weight_terms(query_feat_grad, padded_query, tok_rows),
            weight_terms(key_feat_grad, padded_key, tok_rows),
            weight_terms(value_feat_grad, padded_value, tok_rows),
        ]
    )
    featurizer_grad = lax.psum(partial_terms, "seq") * scale
    return (
        mixed,
        query_grad.astype(jnp.bfloat16),
        key_grad.astype(jnp.bfloat16),
        value_grad.astype(jnp.bfloat16),
        filter_grad,
        featurizer_grad,
    )


LANES = 128
HALO = 16
SPLIT = (TAPS + 1) // 2
PART_ROWS = 16
MESH = pl.DeviceIdType.MESH


def wave_tables(seq_count, tok):
    radix = 2 * seq_count
    full = radix * tok
    col = np.arange(tok)
    unit = 2.0 * np.pi / full
    forward, backward = [], []
    for r in range(seq_count):
        gain = np.full((1, 2 * tok), 1.0 / full)
        if r == 0:
            k = radix * np.arange(tok // 2)
            even = unit * ((k[:, None] * col) % full)
            odd = unit * (((k + seq_count)[:, None] * col) % full)
            none = np.zeros_like(even)
            real = np.block([[np.cos(even), none], [none, np.cos(odd)]])
            imag = np.block([[-np.sin(even), none], [none, -np.sin(odd)]])
            imag[0, :tok] = 1.0 - 2.0 * (col % 2)
            gain *= 2.0
            gain[0, [0, tok]] = 1.0 / full
        else:
            k = radix * np.arange(tok) + r
            angle = unit * ((k[:, None] * col) % full)
            real = np.block([np.cos(angle), np.sin(angle)])
            imag = np.block([-np.sin(angle), np.cos(angle)])
        block = np.concatenate([real, imag])
        forward.append(block)
        backward.append(block.T * gain)
    exact = np.stack([np.stack(forward), np.stack(backward)]).astype(np.float32)
    high = exact.astype(jnp.bfloat16)
    low = (exact - high.astype(np.float32)).astype(jnp.bfloat16)
    return np.stack([high, low])


def plus(a, b):
    return a if b is None else b if a is None else a + b


def minus(a, b):
    return a if b is None else -b if a is None else a - b


def scaled(a, factor):
    if a is None or abs(factor) < 1e-9:
        return None
    if abs(factor - 1.0) < 1e-9:
        return a
    return -a if abs(factor + 1.0) < 1e-9 else a * factor


def rotated(value, angle):
    c, s = math.cos(angle), math.sin(angle)
    re, im = value
    return minus(scaled(re, c), scaled(im, s)), plus(scaled(re, s), scaled(im, c))


def real_dft(values):
    size = len(values)
    if size == 2:
        return [(plus(*values), None), (minus(*values), None)]
    even, odd = real_dft(values[0::2]), real_dft(values[1::2])
    out = [None] * (size // 2 + 1)
    for r in range(size // 4 + 1):
        turned = rotated(odd[r], -2.0 * math.pi * r / size)
        out[size // 2 - r] = (minus(even[r][0], turned[0]), minus(turned[1], even[r][1]))
        out[r] = (plus(even[r][0], turned[0]), plus(even[r][1], turned[1]))
    return out


def real_inverse(spectrum):
    size = 2 * (len(spectrum) - 1)
    if size == 2:
        first, second = spectrum[0][0], spectrum[1][0]
        return [plus(first, second), minus(first, second)]
    even, odd = [], []
    for r in range(size // 4 + 1):
        (re, im), (other_re, other_im) = spectrum[r], spectrum[size // 2 - r]
        if r == 0:
            im, other_im = None, None
        if 4 * r == size:
            even.append((2.0 * re, None))
            odd.append((-2.0 * im, None))
            continue
        even.append((plus(re, other_re), minus(im, other_im)))
        odd.append(
            rotated((minus(re, other_re), plus(im, other_im)), 2.0 * math.pi * r / size)
        )
    out = [None] * size
    out[0::2], out[1::2] = real_inverse(even), real_inverse(odd)
    return out


def split_parts(value):
    high = value.astype(jnp.bfloat16)
    return high, (value - high.astype(jnp.float32)).astype(jnp.bfloat16)


def matmul(left, right):
    return jnp.dot(left, right, preferred_element_type=jnp.float32)


def swapped(value):
    return pltpu.roll(value, LANES // 2, axis=1)


def low_lanes(rows):
    return lax.broadcasted_iota(jnp.int32, (rows, LANES), 1) < LANES // 2


def operator_kernel(
    dims,
    q_ref, k_ref, v_ref, w_hbm, taps_hbm, cot_ref, wave_hbm,
    mixed_ref, qg_ref, kg_ref, vg_ref, fgrad_ref, wgrad_ref,
    ext, w_ref, taps_ref, wave, feat, grads, taps_tx, taps_rx, mg_tx, mg_rx,
    taps_mix, hspec, sig_mix, spec, back, conv_tx, conv_rx,
    filt_tx, filt_rx, part_tx, part_rx, sums_rx,
    load, halo_send, halo_recv, taps_send, taps_recv, mg_send, mg_recv,
    conv_send, conv_recv, filt_send, filt_recv, part_send, part_recv, sum_send, sum_recv,
):
    seq_count, ch_count, tok, width = dims
    count = seq_count * ch_count
    length = seq_count * tok
    tiles = width // LANES
    rows_f = length // count
    half_f = rows_f // 2
    ext_rows = tok + HALO
    f32 = jnp.float32
    seq = lax.axis_index("seq")
    ch = lax.axis_index("ch")
    me = seq * ch_count + ch
    scale = length ** (-0.5)

    def place(flat):
        return lax.div(flat, ch_count), lax.rem(flat, ch_count)

    def peer(step):
        return lax.rem(me + step, count)

    def lane_ds(tile):
        return pl.ds(pl.multiple_of(tile * LANES, LANES), LANES)

    loads = [pltpu.make_async_copy(taps_hbm, taps_ref, load.at[0])]
    for i, ref in enumerate((q_ref, k_ref, v_ref, cot_ref)):
        loads.append(pltpu.make_async_copy(ref, ext.at[i, HALO : HALO + tok], load.at[1 + i]))
    loads.append(pltpu.make_async_copy(w_hbm, w_ref, load.at[5]))
    for i in range(4):
        part = (i % 2, i // 2)
        loads.append(pltpu.make_async_copy(wave_hbm.at[part], wave.at[part], load.at[6 + i]))
    for copy in loads:
        copy.start()

    barrier = pltpu.get_barrier_semaphore()

    @pl.loop(1, count)
    def _(step):
        pl.semaphore_signal(barrier, inc=1, device_id=place(peer(step)), device_id_type=MESH)


    @pl.when(seq == 0)
    def _():
        ext[:, 0:HALO, :] = jnp.zeros((4, HALO, width), jnp.bfloat16)

    @pl.when(seq == seq_count - 1)
    def _():
        ext[:, HALO + tok :, :] = jnp.zeros((4, HALO, width), jnp.bfloat16)

    conv_tx[seq_count - 1, tok:, :] = jnp.zeros((HALO, LANES), jnp.bfloat16)
    low_half = low_lanes(half_f)
    loads[0].wait()

    for tile in range(ch_count * tiles):
        cols = slice(tile * LANES, (tile + 1) * LANES)
        top = taps_ref[0:half_f, cols].astype(f32)
        bottom = taps_ref[half_f:rows_f, cols].astype(f32)
        even_flat = 2 * (tile % tiles) * ch_count + tile // tiles
        taps_tx[even_flat] = jnp.where(low_half, top, swapped(bottom)).astype(jnp.bfloat16)
        taps_tx[even_flat + ch_count] = jnp.where(low_half, swapped(top), bottom).astype(jnp.bfloat16)

    for copy in loads[1:6]:
        copy.wait()

    def mix_gate(to_rows, feats, cot):
        low = low_lanes(to_rows)
        mix = feats[1] * feats[2]
        gate = cot.astype(f32) * feats[0]
        even = jnp.where(low, mix, swapped(gate)).astype(jnp.bfloat16)
        odd = jnp.where(low, swapped(mix), gate).astype(jnp.bfloat16)
        return even, odd

    @pl.loop(0, tiles)
    def _(tile):
        cols = lane_ds(tile)
        parts = []
        for i in range(3):
            raw = ext[i, HALO : HALO + tok, cols].astype(f32)
            total = jnp.zeros((tok - HALO, LANES), f32)
            for lag in range(TAPS):
                total = total + w_ref[i, lag : lag + 1, cols] * raw[HALO - lag : tok - lag]
            feat[i, HALO:tok, cols] = total
            parts.append(total)
        cot = ext[3, 2 * HALO : HALO + tok, cols]
        even, odd = mix_gate(tok - HALO, parts, cot)
        mg_tx[2 * tile, HALO:, :] = even
        mg_tx[2 * tile + 1, HALO:, :] = odd

    pl.semaphore_wait(barrier, count - 1)

    def halo_copy(src, dst, i, to):
        return pltpu.make_async_remote_copy(
            src_ref=src, dst_ref=dst, send_sem=halo_send.at[i], recv_sem=halo_recv.at[i],
            device_id=(to, ch), device_id_type=MESH,
        )

    def up_copy(i):
        return halo_copy(ext.at[i, tok : tok + HALO], ext.at[i, 0:HALO], i, seq + 1)

    def down_copy(i):
        return halo_copy(ext.at[i, HALO : 2 * HALO], ext.at[i, HALO + tok :], 3 + i, seq - 1)

    @pl.when(seq < seq_count - 1)
    def _():
        for i in range(3):
            up_copy(i).start()

    @pl.when(seq > 0)
    def _():
        for i in range(4):
            down_copy(i).start()

    def taps_copy(step):
        to_seq, to_ch = place(peer(step))
        return pltpu.make_async_remote_copy(
            src_ref=taps_tx.at[peer(step)],
            dst_ref=taps_rx.at[me], send_sem=taps_send.at[step], recv_sem=taps_recv.at[step],
            device_id=(to_seq, to_ch), device_id_type=MESH,
        )

    @pl.loop(1, count)
    def _(step):
        taps_copy(step).start()

    taps_rx[me] = taps_tx[me]

    @pl.when(seq > 0)
    def _():
        for i in range(3):
            up_copy(i).wait_recv()

    @pl.when(seq < seq_count - 1)
    def _():
        for i in range(4):
            down_copy(i).wait_recv()


    def mg_copy(to):
        return pltpu.make_async_remote_copy(
            src_ref=mg_tx.at[to], dst_ref=mg_rx.at[seq], send_sem=mg_send.at[to],
            recv_sem=mg_recv.at[seq], device_id=(to, ch), device_id_type=MESH,
        )

    @pl.loop(0, tiles)
    def _(turn):
        tile = lax.rem(turn + lax.div(seq, 2), tiles)
        cols = lane_ds(tile)
        parts = []
        for i in range(3):
            for start in (0, tok):
                raw = ext[i, start : start + 2 * HALO, cols].astype(f32)
                total = jnp.zeros((HALO, LANES), f32)
                for lag in range(TAPS):
                    total = total + w_ref[i, lag : lag + 1, cols] * raw[HALO - lag : 2 * HALO - lag]
                feat[i, start : start + HALO, cols] = total
                if start == 0:
                    parts.append(total)
        even, odd = mix_gate(HALO, parts, ext[3, HALO : 2 * HALO, cols])
        for side, value in ((0, even), (1, odd)):
            to = 2 * tile + side
            mg_tx[to, 0:HALO, :] = value

            @pl.when(to != seq)
            def _():
                mg_copy(to).start()

    mg_rx[seq] = mg_tx[seq]

    @pl.loop(1, count)
    def _(step):
        taps_copy(step).wait_recv()

    for copy in loads[6:8]:
        copy.wait()

    def put(store, rows, spectrum):
        for r in range(seq_count):
            first, second = spectrum[r]
            if r == 0:
                second = spectrum[seq_count][0]
            store(r, rows, first)
            store(r, slice(tok + rows.start, tok + rows.stop), second)

    def store_taps(r, rows, value):
        high = value.astype(jnp.bfloat16)
        wide = high.astype(f32)
        taps_mix[1, r, rows, :] = high
        taps_mix[0, r, rows, :] = jnp.where(low_half, wide, value - wide).astype(jnp.bfloat16)

    nothing = [None] * seq_count
    for j in range(tok // half_f):
        blocks = []
        for m in range(seq_count):
            raw = taps_rx[ch_count * m + j // 2].astype(f32)
            pair = (raw, swapped(raw))
            blocks.append(jnp.where(low_half, pair[j % 2], pair[1 - j % 2]))
        put(store_taps, slice(j * half_f, (j + 1) * half_f), real_dft(blocks + nothing))

    low_tok = low_lanes(tok)
    first_row = lax.broadcasted_iota(jnp.int32, (tok, LANES), 0) == 0
    for r in range(seq_count):
        both = matmul(wave[0, 0, r], taps_mix[0, r])
        value = both + swapped(both) + matmul(wave[1, 0, r], taps_mix[1, r])
        hspec[r, 0:tok, :] = value[:tok]
        upright = jnp.logical_or(low_tok, first_row) if r == 0 else low_tok
        hspec[r, tok:, :] = jnp.where(upright, value[tok:], -value[tok:])


    def from_peer(copy_of, total, mine):
        @pl.loop(0, total)
        def _(source):
            @pl.when(source != mine)
            def _():
                copy_of(source).wait_recv()

    def mg_arrival(source):
        return pltpu.make_async_remote_copy(
            src_ref=mg_tx.at[source], dst_ref=mg_rx.at[source], send_sem=mg_send.at[source],
            recv_sem=mg_recv.at[source], device_id=(source, ch), device_id_type=MESH,
        )

    from_peer(mg_arrival, seq_count, seq)
    for copy in loads[8:]:
        copy.wait()

    def store_signal(r, rows, value):
        high, rest = split_parts(value)
        sig_mix[r, rows, 0:LANES] = high
        sig_mix[r, rows, LANES:] = rest

    for j in range(tok // half_f):
        rows = slice(j * half_f, (j + 1) * half_f)
        blocks = [mg_rx[m, rows, :].astype(f32) for m in range(seq_count)]
        put(store_signal, rows, real_dft(blocks + nothing))

    for r in range(seq_count):
        both = matmul(wave[0, 0, r], sig_mix[r])
        value = both[:, :LANES] + both[:, LANES:] + matmul(wave[1, 0, r], sig_mix[r, :, 0:LANES])
        xr, xi = value[:tok], value[tok:]
        hr, hi = hspec[r, 0:tok, :], hspec[r, tok:, :]
        other_r, other_i = swapped(xr), swapped(xi)
        ii, filt_ii = hi * xi, xi * other_i
        if r == 0:
            pr = hr * xr - jnp.where(first_row, 0.0, ii)
            pi = jnp.where(first_row, ii, hr * xi + hi * xr)
            fr = xr * other_r + jnp.where(first_row, 0.0, filt_ii)
            fi = jnp.where(first_row, filt_ii, xr * other_i - xi * other_r)
        else:
            pr = hr * xr - ii
            pi = hr * xi + hi * xr
            fr = xr * other_r + filt_ii
            fi = xr * other_i - xi * other_r
        for rows, cols, item in (
            (slice(0, tok), slice(0, LANES), pr),
            (slice(tok, 2 * tok), slice(0, LANES), pi),
            (slice(0, tok), slice(LANES, 2 * LANES), fr),
            (slice(tok, 2 * tok), slice(LANES, 2 * LANES), fi),
        ):
            spec[0, r, rows, cols], spec[1, r, rows, cols] = split_parts(item)
        back[r] = (
            matmul(wave[0, 1, r], spec[0, r])
            + matmul(wave[0, 1, r], spec[1, r])
            + matmul(wave[1, 1, r], spec[0, r])
        )


    def conv_copy(to):
        return pltpu.make_async_remote_copy(
            src_ref=conv_tx.at[to], dst_ref=conv_rx.at[seq], send_sem=conv_send.at[to],
            recv_sem=conv_recv.at[seq], device_id=(to, ch), device_id_type=MESH,
        )

    def filt_copy(to):
        return pltpu.make_async_remote_copy(
            src_ref=filt_tx.at[to], dst_ref=filt_rx.at[me], send_sem=filt_send.at[to],
            recv_sem=filt_recv.at[me], device_id=place(to), device_id_type=MESH,
        )

    def joined(get):
        spectrum = [(get(0, 0), None)]
        spectrum += [(get(r, 0), get(r, tok)) for r in range(1, seq_count)]
        return spectrum + [(get(0, tok), None)]

    for j in range(tok // half_f):
        start = j * half_f

        def get(r, offset):
            return back[r, offset + start : offset + start + half_f, 0:LANES]

        outs = real_inverse(joined(get))[:seq_count]
        for m in range(seq_count):
            value = outs[m].astype(jnp.bfloat16)
            conv_tx[m, start : start + half_f, :] = value
            if j == 0 and m > 0:
                conv_tx[m - 1, tok:, :] = value[:HALO]


    @pl.loop(1, seq_count)
    def _(step):
        conv_copy(lax.rem(seq + step, seq_count)).start()

    conv_rx[seq] = conv_tx[seq]

    for j in range(tok // rows_f):
        start = j * rows_f

        def get_pair(r, offset):
            at = offset + start
            top = back[r, at : at + half_f, LANES:]
            bottom = back[r, at + half_f : at + rows_f, LANES:]
            return jnp.where(low_half, top, swapped(bottom))

        outs = real_inverse(joined(get_pair))[:seq_count]
        for m in range(seq_count):
            filt_tx[m * ch_count + j] = (outs[m] * scale).astype(jnp.bfloat16)

    filt_rx[me] = filt_tx[me]

    def conv_arrival(source):
        return pltpu.make_async_remote_copy(
            src_ref=conv_tx.at[source], dst_ref=conv_rx.at[source], send_sem=conv_send.at[source],
            recv_sem=conv_recv.at[source], device_id=(source, ch), device_id_type=MESH,
        )

    from_peer(conv_arrival, seq_count, seq)
    low_ext = low_lanes(ext_rows)
    row_ext = lax.broadcasted_iota(jnp.int32, (ext_rows, LANES), 0)
    keep = jnp.logical_or(row_ext < tok, seq < seq_count - 1)
    def part_copy(to):
        return pltpu.make_async_remote_copy(
            src_ref=part_tx.at[to], dst_ref=part_rx.at[seq], send_sem=part_send.at[to],
            recv_sem=part_recv.at[seq], device_id=(to, ch), device_id_type=MESH,
        )

    @pl.loop(0, tiles)
    def _(tile):
        cols = lane_ds(tile)
        first = jnp.where(keep, conv_rx[2 * tile].astype(f32), 0.0)
        second = jnp.where(keep, conv_rx[2 * tile + 1].astype(f32), 0.0)
        conv = jnp.where(low_ext, first, swapped(second))
        mix_grad = jnp.where(low_ext, swapped(first), second)
        mixed_ref[:, cols] = (feat[0, :tok, cols] * conv[:tok]).astype(jnp.bfloat16)
        terms = (
            ext[3, HALO:, cols].astype(f32) * conv,
            mix_grad * feat[2, :, cols],
            mix_grad * feat[1, :, cols],
        )
        lags = []
        for i in range(3):
            grads[i, :, cols] = terms[i]
            raw = ext[i, :, cols].astype(f32)
            sums = [
                jnp.sum(terms[i][:tok] * raw[HALO - lag : HALO - lag + tok], axis=0, keepdims=True)
                for lag in range(TAPS)
            ]
            lags.append(sums)
        for side in range(2):
            picked = [row for sums in lags for row in sums[side * SPLIT : (side + 1) * SPLIT]]
            picked.append(jnp.zeros((PART_ROWS - len(picked), LANES), f32))
            to = 2 * tile + side
            part_tx[to] = jnp.concatenate(picked, axis=0)

            @pl.when(to != seq)
            def _():
                part_copy(to).start()

            @pl.when(to == seq)
            def _():
                part_rx[to] = part_tx[to]

    @pl.loop(1, count)
    def _(step):
        filt_copy(peer(step)).start()

    @pl.loop(0, tiles)
    def _(tile):
        cols = lane_ds(tile)
        for i, ref in enumerate((qg_ref, kg_ref, vg_ref)):
            term = grads[i, :, cols]
            total = jnp.zeros((tok, LANES), f32)
            for lag in range(TAPS):
                total = total + w_ref[i, lag : lag + 1, cols] * term[lag : lag + tok]
            ref[:, cols] = total.astype(jnp.bfloat16)


    def part_arrival(source):
        return pltpu.make_async_remote_copy(
            src_ref=part_tx.at[source], dst_ref=part_rx.at[source], send_sem=part_send.at[source],
            recv_sem=part_recv.at[source], device_id=(source, ch), device_id_type=MESH,
        )

    from_peer(part_arrival, seq_count, seq)
    own_sum = part_rx[0]
    for source in range(1, seq_count):
        own_sum = own_sum + part_rx[source]
    sums_rx[seq] = own_sum * scale

    def sum_copy(to):
        return pltpu.make_async_remote_copy(
            src_ref=sums_rx.at[seq], dst_ref=sums_rx.at[seq], send_sem=sum_send.at[to],
            recv_sem=sum_recv.at[seq], device_id=(to, ch), device_id_type=MESH,
        )

    @pl.loop(1, seq_count)
    def _(step):
        sum_copy(lax.rem(seq + step, seq_count)).start()


    def filt_arrival(source):
        return pltpu.make_async_remote_copy(
            src_ref=filt_tx.at[source], dst_ref=filt_rx.at[source], send_sem=filt_send.at[source],
            recv_sem=filt_recv.at[source], device_id=place(source), device_id_type=MESH,
        )

    from_peer(filt_arrival, count, me)

    @pl.loop(0, ch_count * tiles)
    def _(tile):
        cols = lane_ds(tile)
        pair = lax.rem(tile, tiles)
        owner = lax.div(tile, tiles)
        first = filt_rx[2 * pair * ch_count + owner].astype(f32)
        second = filt_rx[(2 * pair + 1) * ch_count + owner].astype(f32)
        fgrad_ref[0:half_f, cols] = jnp.where(low_half, first, swapped(second))
        fgrad_ref[half_f:rows_f, cols] = jnp.where(low_half, swapped(first), second)


    def sum_arrival(source):
        return pltpu.make_async_remote_copy(
            src_ref=sums_rx.at[seq], dst_ref=sums_rx.at[source], send_sem=sum_send.at[source],
            recv_sem=sum_recv.at[source], device_id=(source, ch), device_id_type=MESH,
        )

    from_peer(sum_arrival, seq_count, seq)
    for tile in range(tiles):
        cols = slice(tile * LANES, (tile + 1) * LANES)
        for side in range(2):
            rows = min(SPLIT, TAPS - side * SPLIT)
            for i in range(3):
                wgrad_ref[i, side * SPLIT : side * SPLIT + rows, cols] = sums_rx[
                    2 * tile + side, i * rows : (i + 1) * rows
                ]

    @pl.when(seq < seq_count - 1)
    def _():
        for i in range(3):
            up_copy(i).wait_send()

    @pl.when(seq > 0)
    def _():
        for i in range(4):
            down_copy(i).wait_send()

    @pl.loop(1, count)
    def _(step):
        taps_copy(step).wait_send()
        filt_copy(peer(step)).wait_send()

    @pl.loop(1, seq_count)
    def _(step):
        to = lax.rem(seq + step, seq_count)
        mg_copy(to).wait_send()
        conv_copy(to).wait_send()
        part_copy(to).wait_send()
        sum_copy(to).wait_send()


def write_out(*refs):
    half = len(refs) // 2
    for source, target in zip(refs[:half], refs[half:]):
        target[...] = source[...]


def on_device(dims, *args):
    seq_count, ch_count, tok, width = dims
    count = seq_count * ch_count
    length = seq_count * tok
    half_f = length // count // 2
    bf16, f32 = jnp.bfloat16, jnp.float32
    vmem = pl.BlockSpec(memory_space=pltpu.VMEM)
    hbm = pl.BlockSpec(memory_space=pltpu.HBM)
    ext_rows = tok + HALO
    dma = pltpu.SemaphoreType.DMA
    out = jax.ShapeDtypeStruct((tok, width), bf16)
    outs = (
        out, out, out, out,
        jax.ShapeDtypeStruct((length // count, width * ch_count), f32),
        jax.ShapeDtypeStruct((3, TAPS, width), f32),
    )
    waves = wave_tables(seq_count, tok)
    results = pl.pallas_call(
        functools.partial(operator_kernel, dims),
        out_shape=outs,
        in_specs=[hbm] * 7,
        out_specs=(vmem,) * 6,
        scratch_shapes=[
            pltpu.VMEM((4, tok + 2 * HALO, width), bf16),
            pltpu.VMEM((3, TAPS, width), f32),
            pltpu.VMEM((length // count, width * ch_count), bf16),
            pltpu.VMEM(waves.shape, bf16),
            pltpu.VMEM((3, ext_rows, width), f32),
            pltpu.VMEM((3, ext_rows, width), f32),
            pltpu.VMEM((count, half_f, LANES), bf16),
            pltpu.VMEM((count, half_f, LANES), bf16),
            pltpu.VMEM((seq_count, tok, LANES), bf16),
            pltpu.VMEM((seq_count, tok, LANES), bf16),
            pltpu.VMEM((2, seq_count, 2 * tok, LANES), bf16),
            pltpu.VMEM((seq_count, 2 * tok, LANES), f32),
            pltpu.VMEM((seq_count, 2 * tok, 2 * LANES), bf16),
            pltpu.VMEM((2, seq_count, 2 * tok, 2 * LANES), bf16),
            pltpu.VMEM((seq_count, 2 * tok, 2 * LANES), f32),
            pltpu.VMEM((seq_count, ext_rows, LANES), bf16),
            pltpu.VMEM((seq_count, ext_rows, LANES), bf16),
            pltpu.VMEM((count, half_f, LANES), bf16),
            pltpu.VMEM((count, half_f, LANES), bf16),
            pltpu.VMEM((seq_count, PART_ROWS, LANES), f32),
            pltpu.VMEM((seq_count, PART_ROWS, LANES), f32),
            pltpu.VMEM((seq_count, PART_ROWS, LANES), f32),
            dma((10,)), dma((7,)), dma((7,)), dma((count,)), dma((count,)),
            dma((seq_count,)), dma((seq_count,)), dma((seq_count,)), dma((seq_count,)),
            dma((count,)), dma((count,)), dma((seq_count,)), dma((seq_count,)),
            dma((seq_count,)), dma((seq_count,)),
        ],
        compiler_params=pltpu.CompilerParams(
            collective_id=0, has_side_effects=True, vmem_limit_bytes=32 * 1024 * 1024
        ),
    )(*[pltpu.with_memory_space_constraint(value, pltpu.HBM) for value in (*args, waves)])
    return pl.pallas_call(
        write_out, out_shape=outs, in_specs=[vmem] * 6, out_specs=(vmem,) * 6,
        compiler_params=pltpu.CompilerParams(vmem_limit_bytes=8 * 1024 * 1024),
    )(*results)


def block_function(mesh, query_raw, filter_taps):
    seq_count, ch_count = mesh.shape["seq"], mesh.shape["ch"]
    tok, width = query_raw.shape
    length = seq_count * tok
    rows_f = filter_taps.shape[0]
    fits = (
        2 * width == seq_count * LANES
        and seq_count & (seq_count - 1) == 0
        and seq_count >= 4
        and tok == LANES
        and rows_f == 32
        and tok == ch_count * rows_f
    )
    if fits:
        return functools.partial(on_device, (seq_count, ch_count, tok, width))
    return on_device_large


def solution(mesh):
    def body(*args):
        return block_function(mesh, args[0], args[4])(*args)

    return jax.shard_map(
        body,
        mesh=mesh,
        in_specs=(
            P("seq", "ch"),
            P("seq", "ch"),
            P("seq", "ch"),
            P(None, None, "ch"),
            P(("seq", "ch"), None),
            P("seq", "ch"),
        ),
        out_specs=(
            P("seq", "ch"),
            P("seq", "ch"),
            P("seq", "ch"),
            P("seq", "ch"),
            P(("seq", "ch"), None),
            P(None, None, "ch"),
        ),
        check_vma=False,
    )
```
